32 devices in a mesh: rx: 4 (over z), ry: 8 (over y, x, core).
Axes of the slice: x: 2, y: 2, z: 4, core: 2. Of those that a mesh axis runs over, the one named last changes fastest.
Arguments:
- features: bfloat16 [256, 64, 512], P(('rx', 'ry')), may hold values from -6 to 6
- grad_out: bfloat16 [256, 64, 512], P(('rx', 'ry')), may hold values from -6 to 6
- weights: bfloat16 [27, 64, 64], replicated, may hold values from -0.15625 to 0.15625
- live_count: int32 [32], P(('rx', 'ry')), may hold values from 0 to 8, as said below
- neighbor: int32 [256, 6], P(('rx', 'ry')), may hold values from -1 to 23, as said below
- send_list: int32 [128, 4], P(('rx', 'ry')), may hold values from -1 to 7, as said below
Outputs:
- output: bfloat16 [256, 64, 512], P(('rx', 'ry'))
- grad_features: bfloat16 [256, 64, 512], P(('rx', 'ry'))
- grad_weights: float32 [27, 64, 64], replicated
The draws below stay inside these ranges and needn't reach their ends.
Inputs may be any that keep to these rules, and one draw needn't show every extreme that they name: A device's occupied bricks take its first live_count slots; some device is full. `neighbor`: only live slots have entries other than -1. Entries of 8 or more stand only in columns 0 to 3, equal 8 + s * 4 + k in column s, and never point beyond the grid of devices. Sides 4 and 5 are always within the device. Adjacency is mutual: a brick is its neighbour's neighbour on the opposite side, and each received face slot of a side is used by at most one brick. `send_list`: row 4 d + t lists distinct live slots of device d, their face t going to the device beside d on side t; used entries come first, then -1.
All inputs are finite; a program needn't handle non-finite values.
Results may differ from the reference program's by a relative error of at most 0.0025.
Values may be sent and summed in bfloat16 or wider, within the bound.
A program may use at most 64 MiB of HBM per device.

```python
import jax
import jax.numpy as jnp
from jax import lax

C = 64
RB = 2
H = 2
B_DEV = 8
CAP = 4
BRICKS = 256
N_RX = 4
N_RY = 8


def shift_low(values, axis):
    first = jnp.zeros_like(lax_take(values, axis, 0, 1))
    rest = lax_take(values, axis, 0, values.shape[axis] - 1)
    return jnp.concatenate([first, rest], axis=axis)


def shift_high(values, axis):
    last = jnp.zeros_like(lax_take(values, axis, 0, 1))
    rest = lax_take(values, axis, 1, values.shape[axis] - 1)
    return jnp.concatenate([rest, last], axis=axis)


def lax_take(values, axis, start, length):
    return jnp.take(values, jnp.arange(start, start + length), axis=axis)


def local_value(occupied, slot_rank):
    return jnp.where(occupied == 1, slot_rank, -1)


def pair_keys(pairs):
    shape = pairs.shape
    flat_pairs = pairs.reshape(shape[0], shape[1], -1)
    return (jnp.cumsum(flat_pairs, axis=-1) - 1).reshape(shape).astype(jnp.int32)


def build_bricks(key):
    subkeys = jax.random.split(jax.random.fold_in(key, 4242), 4)
    positions = RB * RB * H
    devices = N_RX * N_RY
    fill_rate = jax.random.randint(subkeys[0], (N_RX, N_RY), 40, 101)
    full_row = jax.random.randint(subkeys[1], (), 0, N_RX - 1)
    full_col = jax.random.randint(subkeys[2], (), 0, N_RY - 1)
    grid_rows = jnp.arange(N_RX)[:, None]
    grid_cols = jnp.arange(N_RY)[None, :]
    full = (grid_rows == full_row) & (grid_cols == full_col) | (grid_rows == full_row + 1) & (grid_cols == full_col) | (grid_rows == full_row) & (grid_cols == full_col + 1)
    fill_rate = jnp.where(full, 101, fill_rate)
    rolls = jax.random.randint(subkeys[3], (N_RX, N_RY, RB, RB, H), 0, 100)
    occupied = (rolls < fill_rate[:, :, None, None, None]).astype(jnp.int32)
    flat_occ = occupied.reshape(N_RX, N_RY, positions)
    slot_rank = (jnp.cumsum(flat_occ, axis=-1) - 1).reshape(occupied.shape).astype(jnp.int32)
    count = flat_occ.sum(-1).reshape(devices).astype(jnp.int32)
    pair_x = occupied[:-1, :, RB - 1] * occupied[1:, :, 0]
    key_x = pair_keys(pair_x)
    pad_x = jnp.zeros((1, N_RY, RB, H), jnp.int32)
    pair_x_low = jnp.concatenate([pad_x, pair_x], 0)
    key_x_low = jnp.concatenate([pad_x, key_x], 0)
    pair_x_high = jnp.concatenate([pair_x, pad_x], 0)
    key_x_high = jnp.concatenate([key_x, pad_x], 0)
    pair_y = occupied[:, :-1, :, RB - 1] * occupied[:, 1:, :, 0]
    key_y = pair_keys(pair_y)
    pad_y = jnp.zeros((N_RX, 1, RB, H), jnp.int32)
    pair_y_low = jnp.concatenate([pad_y, pair_y], 1)
    key_y_low = jnp.concatenate([pad_y, key_y], 1)
    pair_y_high = jnp.concatenate([pair_y, pad_y], 1)
    key_y_high = jnp.concatenate([key_y, pad_y], 1)
    index_x = jnp.arange(RB)[:, None, None]
    index_y = jnp.arange(RB)[None, :, None]
    side_zero = jnp.where(index_x > 0, local_value(shift_low(occupied, 2), shift_low(slot_rank, 2)), jnp.where(pair_x_low[:, :, None] == 1, positions + key_x_low[:, :, None], -1))
    side_one = jnp.where(index_x < RB - 1, local_value(shift_high(occupied, 2), shift_high(slot_rank, 2)), jnp.where(pair_x_high[:, :, None] == 1, positions + CAP + key_x_high[:, :, None], -1))
    side_two = jnp.where(index_y > 0, local_value(shift_low(occupied, 3), shift_low(slot_rank, 3)), jnp.where(pair_y_low[:, :, :, None] == 1, positions + 2 * CAP + key_y_low[:, :, :, None], -1))
    side_three = jnp.where(index_y < RB - 1, local_value(shift_high(occupied, 3), shift_high(slot_rank, 3)), jnp.where(pair_y_high[:, :, :, None] == 1, positions + 3 * CAP + key_y_high[:, :, :, None], -1))
    side_four = local_value(shift_low(occupied, 4), shift_low(slot_rank, 4))
    side_five = local_value(shift_high(occupied, 4), shift_high(slot_rank, 4))
    sides = jnp.stack([side_zero, side_one, side_two, side_three, side_four, side_five], axis=-1)
    sides = jnp.where(occupied[..., None] == 1, sides, -1).astype(jnp.int32)
    slot_of = jnp.where(occupied == 1, slot_rank, positions).reshape(devices, positions)
    device_ids = jnp.broadcast_to(jnp.arange(devices)[:, None], (devices, positions))
    table = jnp.full((devices, positions + 1, 6), -1, jnp.int32)
    table = table.at[device_ids, slot_of].set(sides.reshape(devices, positions, 6))
    neighbor = table[:, :positions].reshape(devices * positions, 6)

    def sender(pairs, keys, slots):
        target = jnp.where(pairs == 1, keys, CAP).reshape(devices, -1)
        owners = jnp.broadcast_to(jnp.arange(devices)[:, None], target.shape)
        listed = jnp.full((devices, CAP + 1), -1, jnp.int32)
        listed = listed.at[owners, target].set(slots.reshape(devices, -1).astype(jnp.int32))
        return listed[:, :CAP]
    send_zero = sender(pair_x_low, key_x_low, slot_rank[:, :, 0])
    send_one = sender(pair_x_high, key_x_high, slot_rank[:, :, RB - 1])
    send_two = sender(pair_y_low, key_y_low, slot_rank[:, :, :, 0])
    send_three = sender(pair_y_high, key_y_high, slot_rank[:, :, :, RB - 1])
    send_list = jnp.stack([send_zero, send_one, send_two, send_three], axis=1).reshape(devices * 4, CAP)
    return (count, neighbor, send_list)


def draw_live_count(key, part):
    return build_bricks(key)[0]


def draw_neighbor(key, part):
    return build_bricks(key)[1]


def draw_send_list(key, part):
    return build_bricks(key)[2]


def level_of(stream_key, dims, cuts, smallest, high):
    def one(position, shards_of):
        steps = jax.random.uniform(jax.random.fold_in(jax.random.fold_in(stream_key, 6), position), (shards_of,), jnp.float32, smallest / len(cuts), high / len(cuts))
        return jnp.repeat(jnp.exp(steps), dims[position] // shards_of).reshape((-1,) + (1,) * (len(dims) - position - 1))

    level = one(*cuts[0])
    for cut in cuts[1:]:
        level = level * one(*cut)
    return level


def gaussian(rng, shape, width, limit, shards=(), held_as=jnp.bfloat16):
    level = level_of(rng, shape, shards, -0.22, 0.18) if shards else 1.0
    values = jax.random.normal(rng, shape, jnp.float32) * width * level
    return jnp.minimum(jnp.maximum(values, -limit), limit).astype(held_as)


def setup_inputs(seed: int = 0) -> dict:
    arg_keys = jax.random.split(jax.random.key(seed), 7)
    return {
        "features": gaussian(arg_keys[0], (BRICKS, C, 512), 1.0, 6.0, ((0, 32),)),
        "grad_out": gaussian(arg_keys[1], (BRICKS, C, 512), 1.0, 6.0, ((0, 32),)),
        "weights": gaussian(arg_keys[2], (27, C, C), (27 * C) ** -0.5, 0.15625),
        "live_count": draw_live_count(jax.random.fold_in(arg_keys[6], 71), 0),
        "neighbor": draw_neighbor(jax.random.fold_in(arg_keys[6], 71), 0),
        "send_list": draw_send_list(jax.random.fold_in(arg_keys[6], 71), 0),
    }


def face_of(cube, s):
    n, c = (cube.shape[0], cube.shape[1])
    if s == 0:
        layer = cube[:, :, 0]
    elif s == 1:
        layer = cube[:, :, 7]
    elif s == 2:
        layer = cube[:, :, :, 0]
    elif s == 3:
        layer = cube[:, :, :, 7]
    elif s == 4:
        layer = cube[:, :, :, :, 0]
    else:
        layer = cube[:, :, :, :, 7]
    return layer.reshape(n, c, 64)

def halo_index(s):
    every = slice(None)
    within = slice(1, 9)
    table = [(every, every, 0, within, within), (every, every, 9, within, within), (every, every, within, 0, within), (every, every, within, 9, within), (every, every, within, within, 0), (every, every, within, within, 9)]
    return table[s]

def face_index(s):
    every = slice(None)
    table = [(every, every, 0), (every, every, 7), (every, every, every, 0), (every, every, every, 7), (every, every, every, every, 0), (every, every, every, every, 7)]
    return table[s]

def put_halo(bordered_volume, s, layer):
    n, c = (bordered_volume.shape[0], bordered_volume.shape[1])
    return bordered_volume.at[halo_index(s)].set(layer.reshape(n, c, 8, 8))

def take_halo(bordered_volume, s):
    n, c = (bordered_volume.shape[0], bordered_volume.shape[1])
    return bordered_volume[halo_index(s)].reshape(n, c, 64)

def add_face(cube, s, layer):
    n, c = (cube.shape[0], cube.shape[1])
    return cube.at[face_index(s)].add(layer.reshape(n, c, 8, 8))

def window_stack(bordered_volume):
    n, c = (bordered_volume.shape[0], bordered_volume.shape[1])
    shifted = []
    for a in range(3):
        for b in range(3):
            for d in range(3):
                shifted.append(bordered_volume[:, :, a:a + 8, b:b + 8, d:d + 8].reshape(n, c, 512))
    return jnp.concatenate(shifted, axis=1)

def convolve(bordered_volume, weight_matrix):
    return jnp.einsum('ah,thp->tap', weight_matrix, window_stack(bordered_volume), precision=lax.Precision.HIGHEST)

def reference(features, grad_out, weights, live_count, neighbor, send_list):
    devices = N_RX * N_RY
    total = features.shape[0]
    chans = features.shape[1]
    device = jnp.arange(total, dtype=jnp.int32) // B_DEV
    grid_row = device // N_RY
    grid_col = device % N_RY
    live_mask = jnp.arange(total, dtype=jnp.int32) % B_DEV < live_count[device]
    feat_live = jnp.where(live_mask[:, None, None], features, jnp.zeros_like(features))
    grad_live = jnp.where(live_mask[:, None, None], grad_out, jnp.zeros_like(grad_out))
    sources = []
    for s in range(6):
        entry_val = neighbor[:, s]
        source = jnp.where((entry_val >= 0) & (entry_val < B_DEV), device * B_DEV + entry_val, total)
        if s < 4:
            k = jnp.clip((entry_val - B_DEV) % CAP, 0, CAP - 1)
            peer_row = jnp.clip(grid_row + [-1, 1, 0, 0][s], 0, N_RX - 1)
            peer_col = jnp.clip(grid_col + [0, 0, -1, 1][s], 0, N_RY - 1)
            peer_dev = peer_row * N_RY + peer_col
            slot_index = send_list[peer_dev * 4 + (s ^ 1), k]
            remote = (entry_val >= B_DEV) & (slot_index >= 0)
            source = jnp.where(remote, peer_dev * B_DEV + slot_index, source)
        sources.append(source.astype(jnp.int32))
    source = jnp.stack(sources, axis=1)
    feat_cube = feat_live.reshape(total, chans, 8, 8, 8)
    faces = jnp.stack([face_of(feat_cube, s) for s in range(6)], axis=1)
    faces = jnp.concatenate([faces, jnp.zeros((1, 6, chans, 64), features.dtype)], axis=0)
    weight_matrix = weights.astype(jnp.float32).transpose(1, 0, 2).reshape(chans, 27 * chans)

    def one_device(inputs):
        feat_block, gradient_tile, block_src = inputs
        bordered_volume = jnp.pad(feat_block.reshape(B_DEV, chans, 8, 8, 8), ((0, 0), (0, 0), (1, 1), (1, 1), (1, 1)))
        for s in range(6):
            bordered_volume = put_halo(bordered_volume, s, faces[block_src[:, s], s ^ 1])
        output, pull_back = jax.vjp(convolve, bordered_volume.astype(jnp.float32), weight_matrix)
        grad_pad, grad_w = pull_back(gradient_tile.astype(jnp.float32))
        interior = grad_pad[:, :, 1:9, 1:9, 1:9].reshape(B_DEV, chans, 512)
        returned = jnp.stack([take_halo(grad_pad, s) for s in range(6)], axis=1)
        return (output.astype(jnp.bfloat16), interior, returned, grad_w)
    results = lax.map(one_device, (feat_live.reshape(devices, B_DEV, chans, 512), grad_live.reshape(devices, B_DEV, chans, 512), source.reshape(devices, B_DEV, 6)))
    output = results[0].reshape(total, chans, 512)
    interior = results[1].reshape(total, chans, 512)
    returned = results[2].reshape(total, 6, chans, 64)
    grad_w = lax.optimization_barrier(jnp.sum(results[3], axis=0))
    collected = jnp.zeros((total + 1, 6, chans, 64), jnp.float32)
    for s in range(6):
        collected = collected.at[source[:, s], s ^ 1].add(returned[:, s])
    grad_cube = interior.reshape(total, chans, 8, 8, 8)
    for s in range(6):
        grad_cube = add_face(grad_cube, s, collected[:total, s])
    output = jnp.where(live_mask[:, None, None], output, jnp.zeros_like(output))
    grad_features = jnp.where(live_mask[:, None, None], grad_cube.reshape(total, chans, 512), 0.0).astype(jnp.bfloat16)
    grad_weights = grad_w.reshape(chans, 27, chans).transpose(1, 0, 2) * (512.0 * total) ** (-0.5)
    return (output, grad_features, grad_weights)
```

```python
import functools

import jax
import jax.numpy as jnp
from jax import lax
from jax.experimental import pallas as pl
from jax.experimental.pallas import tpu as pltpu
from jax.sharding import PartitionSpec as P

MESH = pl.DeviceIdType.MESH
ROWS = 1024
F32, BF16 = jnp.float32, jnp.bfloat16


def dot(x, y):
    return jnp.dot(x, y, preferred_element_type=F32)


def low_lanes(shape):
    return lax.broadcasted_iota(jnp.int32, shape, len(shape) - 1) < 64


def put_window(ref, g, at, mid, low, high):
    rows = mid.shape[0] * 8
    mid, low, high = (v.reshape(rows, 128) for v in (mid, low, high))
    first = low_lanes((rows, 128))
    ref[g, at : at + rows, 0:128] = jnp.where(first, low, pltpu.roll(mid, 64, 1)).astype(BF16)
    ref[g, at : at + rows, 128:256] = high.astype(BF16)
    ref[g, at : at + rows, 256:384] = jnp.where(first, pltpu.roll(low, 64, 1), mid).astype(BF16)


def main_kernel(
    n_rx, n_ry, scale, conv_at,
    live_ref, list_ref, nb_ref, feat_ref, grad_ref, w_ref,
    out_ref, gf_ref, whole,
    t_ref, face_ref, recv_ref, wf_ref, wb_ref, xm_ref, xy_ref, lhs_ref, lhsx_ref, lhsf_ref, acc,
    dw, got0, src1, got1, src2, got2, part,
    face_send, face_recv, send_sem, sem0, sem1, sem2, sem3, sem4, sem5,
):
    slots = feat_ref.shape[0]
    cap = recv_ref.shape[1]
    row, col = lax.axis_index("rx"), lax.axis_index("ry")
    half, par = n_ry // 2, lax.rem(col, 2)
    me = col // 2
    partner = (row, me * 2 + 1 - par)
    others = [lax.rem(me + d, half) for d in range(1, half)]
    rows = [lax.rem(row + d, n_rx) for d in range(1, n_rx)]
    sides = [
        (row > 0, (row - 1, col)),
        (row < n_rx - 1, (row + 1, col)),
        (col > 0, (row, col - 1)),
        (col < n_ry - 1, (row, col + 1)),
    ]

    barrier = pltpu.get_barrier_semaphore()
    for d in range(1, n_ry):
        peer = (row, lax.rem(col + d, n_ry))
        pl.semaphore_signal(barrier, inc=1, device_id=peer, device_id_type=MESH)
    for r in rows:
        pl.semaphore_signal(barrier, inc=1, device_id=(r, col), device_id_type=MESH)

    def pack(g, carry):
        both = jnp.concatenate([feat_ref[g], grad_ref[g]], axis=0).astype(F32)
        cells = jnp.where(g < live_ref[0], jnp.transpose(both), 0.0)
        t_ref[g] = cells.reshape(8, 8, 8, 128)
        return carry

    lax.fori_loop(0, slots, pack, 0)
    for t in range(4):
        for k in range(cap):
            slot = list_ref[t, k]
            e = jnp.maximum(slot, 0)
            if t < 2:
                face = t_ref[e, 0 if t == 0 else 7]
            else:
                face = t_ref[e, :, 0 if t == 2 else 7]
            face = jnp.where(slot >= 0, face, 0.0)
            face_ref[t, k] = face.reshape(64, 128).astype(BF16)
    pl.semaphore_wait(barrier, n_ry + n_rx - 2)

    def copy(src, dst, ssem, rsem, peer):
        return pltpu.make_async_remote_copy(
            src_ref=src, dst_ref=dst, send_sem=ssem, recv_sem=rsem,
            device_id=peer, device_id_type=MESH,
        )

    def swap(t, into, peer):
        return copy(face_ref.at[t], recv_ref.at[into], face_send.at[t], face_recv.at[into], peer)

    for t, (there, peer) in enumerate(sides):

        @pl.when(there)
        def _():
            swap(t, t ^ 1, peer).start()

        @pl.when(jnp.logical_not(there))
        def _():
            recv_ref[t] = jnp.zeros(recv_ref.shape[1:], recv_ref.dtype)

    acc[...] = jnp.zeros_like(acc)
    xy_ref[...] = jnp.zeros_like(xy_ref)
    level = lax.broadcasted_iota(jnp.int32, (64, 8, 128), 1)

    def inner(p, carry):
        lane = lax.broadcasted_iota(jnp.int32, (64, 512), 1) % 64
        edges = []
        for h in range(2):
            g = 2 * p + h
            grads = jnp.where(g < live_ref[0], grad_ref[g].astype(F32), 0.0)

            def turned(shift):
                cut = [grads[:, 128 * q : 128 * q + 128] for q in range(4)]
                return jnp.concatenate([pltpu.roll(v, shift, 1) for v in cut], axis=1)

            ahead = jnp.where(lane < 56, turned(120), 0.0)
            behind = jnp.where(lane >= 8, turned(8), 0.0)
            lhs = jnp.concatenate([ahead, grads, behind], axis=0)
            lhs_ref[g] = lhs.astype(BF16)
            edges.append((lhs[:, 0:128], lhs[:, 384:512]))
            own = t_ref[g]
            ends = jnp.concatenate([own[:, 0:1], own[:, 7:8]], axis=1).reshape(128, 128)
            ends = jnp.transpose(ends)[64:128]
            which = lax.broadcasted_iota(jnp.int32, (64, 128), 1) % 16 < 8
            lhsf_ref[g] = jnp.concatenate(
                [jnp.where(which, ends, 0.0), jnp.where(which, 0.0, ends)], axis=0
            ).astype(BF16)

            mid = own.reshape(64, 8, 128)
            below, above = nb_ref[g, 4], nb_ref[g, 5]
            under = t_ref[jnp.clip(below, 0, slots - 1)].reshape(64, 8, 128)
            over = t_ref[jnp.clip(above, 0, slots - 1)].reshape(64, 8, 128)
            under = jnp.where(below >= 0, under, 0.0)
            over = jnp.where(above >= 0, over, 0.0)
            low = pltpu.roll(jnp.where(level == 7, under, mid), 1, 1)
            high = pltpu.roll(jnp.where(level == 0, over, mid), 7, 1)
            put_window(xm_ref, g, 64, mid, low, high)
            xm_ref[g, 0:64] = jnp.zeros((64, 384), BF16)
            xm_ref[g, 576:640] = jnp.zeros((64, 384), BF16)
            for a in range(3):
                acc[a] += dot(lhs_ref[g], xm_ref[g, 64 * a : 64 * a + 512, 0:256])
        first = low_lanes((192, 128))
        (low0, low1), (high0, high1) = edges
        lhsx_ref[0, p] = jnp.where(first, low0, pltpu.roll(high0, 64, 1)).astype(BF16)
        lhsx_ref[1, p] = jnp.where(first, pltpu.roll(low1, 64, 1), high1).astype(BF16)
        return carry

    lax.fori_loop(0, slots // 2, inner, 0)

    gap = jnp.zeros((64, 64), F32)
    wide = jnp.zeros((64, 256), BF16)
    for a in range(3):
        wf_ref[a, 192:256] = wide
        wb_ref[a, 0:64] = wide
        for c in range(3):
            front = [w_ref[9 * a + 3 * b + c].astype(F32) for b in range(3)]
            block = jnp.transpose(jnp.concatenate(front + [gap], axis=0))
            wf_ref[a, 64 * c : 64 * c + 64] = block.astype(BF16)
            back = [w_ref[26 - 9 * a - 3 * b - c].astype(F32) for b in range(3)]
            block = jnp.concatenate([back[1], back[0], gap, back[2]], axis=1)
            at = 64 * (2, 3, 1)[c]
            wb_ref[a, at : at + 64] = block.astype(BF16)

    for t, (there, peer) in enumerate(sides):

        @pl.when(there)
        def _():
            swap(t, t ^ 1, peer).wait_send()
            swap(t, t, peer).wait_recv()

    def faces(g, carry):
        got = []
        for s in range(4):
            entry = nb_ref[g, s]
            e = jnp.clip(entry, 0, slots - 1)
            k = jnp.maximum(entry - slots, 0) % cap
            layer = 7 if s % 2 == 0 else 0
            local = t_ref[e, layer] if s < 2 else t_ref[e, :, layer]
            far = recv_ref[s, k].astype(F32).reshape(8, 8, 128)
            got.append(jnp.where(entry >= slots, far, jnp.where(entry >= 0, local, 0.0)))

        def around(mid):
            at = lax.broadcasted_iota(jnp.int32, mid.shape, 1)
            low = pltpu.roll(jnp.where(at == 7, 0.0, mid), 1, 1)
            high = pltpu.roll(jnp.where(at == 0, 0.0, mid), 7, 1)
            return mid, low, high

        put_window(xm_ref, g, 0, *around(got[0]))
        put_window(xm_ref, g, 576, *around(got[1]))
        both = jnp.concatenate([got[2][:, None], got[3][:, None]], axis=1).reshape(16, 8, 128)
        put_window(xy_ref, g, 16, *around(both))
        return carry

    lax.fori_loop(0, slots, faces, 0)

    pairs = slots // 2
    for s, a, at in ((0, 0, 0), (1, 2, 576)):
        lhs = jnp.concatenate([lhsx_ref[s, p] for p in range(pairs)], axis=1)
        rhs = jnp.concatenate([xm_ref[g, at : at + 64, 0:256] for g in range(slots)], axis=0)
        acc[a] += dot(lhs, rhs)
    lhs = jnp.concatenate([lhsf_ref[g] for g in range(slots)], axis=1)
    for a in range(3):
        rhs = [xy_ref[g, 16 * a : 16 * a + 128, 0:256] for g in range(slots)]
        more = dot(lhs, jnp.concatenate(rhs, axis=0))
        acc[a, 0:64] += more[0:64]
        acc[a, 128:192] += more[64:128]

    size = ROWS // n_ry
    piece = size // n_rx
    flat = acc[...].reshape(576, 256)
    rest = jnp.concatenate([flat[320:576, 128:256], jnp.zeros((64, 128), F32)], axis=0)
    third = jnp.where(low_lanes((320, 128)), flat[0:320, 128:256], pltpu.roll(rest, 64, 1))
    flat = jnp.concatenate([flat[:, 0:128], third, jnp.zeros((ROWS - 896, 128), F32)], axis=0)
    dw[...] = flat.reshape(half, 2, size, 128)

    def conv(g, carry):
        yf = yb = zf = zb = None
        for a in range(3):
            m = xm_ref[g, 64 * a : 64 * a + 512]
            y = xy_ref[g, 16 * a : 16 * a + 128]
            new = [
                dot(m[:, 0:256], wf_ref[a]), dot(m[:, 128:384], wb_ref[a]),
                dot(y[:, 0:256], wf_ref[a]), dot(y[:, 128:384], wb_ref[a]),
            ]
            if a:
                yf, yb, zf, zb = yf + new[0], yb + new[1], zf + new[2], zb + new[3]
            else:
                yf, yb, zf, zb = new
        yf, yb = yf.reshape(8, 8, 8, 256), yb.reshape(8, 8, 8, 256)
        zf, zb = zf.reshape(8, 2, 8, 256), zb.reshape(8, 2, 8, 256)

        def before(y, z):
            return jnp.concatenate([z[:, 0:1, :, 0:128], y[:, 0:7, :, 0:128]], axis=1)

        def after(y, z):
            return jnp.concatenate([y[:, 1:8, :, 128:256], z[:, 1:2, :, 128:256]], axis=1)

        first = low_lanes((8, 8, 8, 128))
        swapped = jnp.where(first, yb[..., 0:128], yf[..., 0:128])
        total = jnp.where(first, before(yf, zf), before(yb, zb))
        total += after(yf, zf) + after(yb, zb)
        total = total.reshape(512, 128) + pltpu.roll(swapped.reshape(512, 128), 64, 1)
        total = jnp.where(g < live_ref[0], total, 0.0)
        flat = jnp.transpose(total).astype(BF16)
        out_ref[g] = flat[0:64]
        gf_ref[g] = flat[64:128]
        return carry

    def run(n):
        lo, hi = conv_at[n], conv_at[n + 1]
        if hi > lo:
            lax.fori_loop(lo, hi, conv, 0)

    sent = []

    def send(src, dst, stage, n, rsem, peer):
        x = copy(src, dst, send_sem.at[stage, n], rsem, peer)
        x.start()
        sent.append(x)

    def arrived(src, dst, stage, n, rsem, peer):
        copy(src, dst, send_sem.at[stage, n], rsem, peer).wait_recv()

    order = others + [me]
    for n, c in enumerate(order):
        send(dw.at[c, 1 - par], got0.at[c], 0, n, sem0.at[c], partner)
    run(0)
    for n, c in enumerate(order):
        arrived(dw.at[c, 1 - par], got0.at[c], 0, n, sem0.at[c], partner)
        src1[c] = dw[c, par] + got0[c]
        if n < half - 1:
            send(src1.at[c], got1.at[me], 1, n, sem1.at[me], (row, 2 * c + par))
    run(1)
    mine = src1[me]
    for n, c in enumerate(reversed(others)):
        arrived(src1.at[c], got1.at[c], 1, n, sem1.at[c], (row, 2 * c + par))
        mine += got1[c]
    src2[...] = mine.reshape(n_rx, piece, 128)
    for n, r in enumerate(rows):
        send(src2.at[r], got2.at[row], 2, n, sem2.at[row], (r, col))
    run(2)
    small = src2[row]
    for n, r in enumerate(reversed(rows)):
        arrived(src2.at[r], got2.at[r], 2, n, sem2.at[r], (r, col))
        small += got2[r]

    part[row] = (small * scale).astype(part.dtype)
    for n, r in enumerate(rows):
        send(part.at[row], part.at[row], 3, n, sem3.at[row], (r, col))
    run(3)
    for n, r in enumerate(reversed(rows)):
        arrived(part.at[r], part.at[r], 3, n, sem3.at[r], (r, col))
    for n, c in enumerate(others):
        send(part, whole.at[me, par], 4, n, sem4.at[me], (row, 2 * c + par))
    send(part, whole.at[me, par], 5, half - 1, sem5.at[me], partner)
    whole[me, par] = part[...]
    run(4)
    for n, c in enumerate(reversed(others)):
        arrived(part, whole.at[c, par], 4, n, sem4.at[c], (row, 2 * c + par))
        send(whole.at[c, par], whole.at[c, par], 5, n, sem5.at[c], partner)
    run(5)
    for n, c in enumerate(order):
        arrived(part, whole.at[c, 1 - par], 5, n, sem5.at[c], partner)
    for x in sent:
        x.wait_send()


def finish_kernel(packed_ref, out_ref, gf_ref, dw_ref, out, gf):
    full = packed_ref[...].astype(F32).reshape(ROWS, 128)
    for n in range(9):
        pair = full[64 * n : 64 * n + 64]
        dw_ref[3 * n] = pair[:, 0:64]
        dw_ref[3 * n + 1] = pair[:, 64:128]
        at, half = 576 + 64 * (n % 5), 64 * (n // 5)
        dw_ref[3 * n + 2] = full[at : at + 64, half : half + 64]
    out[...] = out_ref[...]
    gf[...] = gf_ref[...]


def body(features, grad_out, weights, live_count, neighbor, send_list):
    slots, channels = features.shape[0], features.shape[1]
    cap = send_list.shape[1]
    n_rx, n_ry = lax.axis_size("rx"), lax.axis_size("ry")
    vmem = pl.BlockSpec(memory_space=pltpu.VMEM)
    smem = pl.BlockSpec(memory_space=pltpu.SMEM)
    scale = (512.0 * slots * n_rx * n_ry) ** (-0.5)
    size = ROWS // n_ry
    piece = size // n_rx
    half = n_ry // 2
    most = max(n_rx, half)
    dma = pltpu.SemaphoreType.DMA
    conv_at = [n * slots // 8 for n in (0, 1, 4, 6, 7, 8, 8)]

    output, grad_features, packed = pl.pallas_call(
        functools.partial(main_kernel, n_rx, n_ry, scale, conv_at),
        out_shape=(
            jax.ShapeDtypeStruct(features.shape, BF16),
            jax.ShapeDtypeStruct(features.shape, BF16),
            jax.ShapeDtypeStruct((half, 2, n_rx, piece, 128), BF16),
        ),
        in_specs=[smem, smem, smem, vmem, vmem, vmem],
        out_specs=(vmem, vmem, vmem),
        scratch_shapes=[
            pltpu.VMEM((slots, 8, 8, 8, 128), F32),
            pltpu.VMEM((4, cap, 64, 128), BF16),
            pltpu.VMEM((4, cap, 64, 128), BF16),
            pltpu.VMEM((3, 256, 256), BF16),
            pltpu.VMEM((3, 256, 256), BF16),
            pltpu.VMEM((slots, 640, 384), BF16),
            pltpu.VMEM((slots, 160, 384), BF16),
            pltpu.VMEM((slots, 192, 512), BF16),
            pltpu.VMEM((2, slots // 2, 192, 128), BF16),
            pltpu.VMEM((slots, 128, 128), BF16),
            pltpu.VMEM((3, 192, 256), F32),
            pltpu.VMEM((half, 2, size, 128), F32),
            pltpu.VMEM((half, size, 128), F32),
            pltpu.VMEM((half, size, 128), F32),
            pltpu.VMEM((half, size, 128), F32),
            pltpu.VMEM((n_rx, piece, 128), F32),
            pltpu.VMEM((n_rx, piece, 128), F32),
            pltpu.VMEM((n_rx, piece, 128), BF16),
            dma((4,)), dma((4,)), dma((6, most)),
            dma((half,)), dma((half,)), dma((n_rx,)), dma((n_rx,)), dma((half,)), dma((half,)),
        ],
        compiler_params=pltpu.CompilerParams(collective_id=0, has_side_effects=True),
        name="main",
    )(live_count, send_list, neighbor, features, grad_out, weights)

    grad_weights, output, grad_features = pl.pallas_call(
        finish_kernel,
        out_shape=(
            jax.ShapeDtypeStruct((27, channels, channels), F32),
            jax.ShapeDtypeStruct(features.shape, BF16),
            jax.ShapeDtypeStruct(features.shape, BF16),
        ),
        in_specs=[vmem, vmem, vmem],
        out_specs=(vmem, vmem, vmem),
        name="finish",
    )(packed, output, grad_features)
    return output, grad_features, grad_weights


def solution(mesh):
    placed = (
        P(("rx", "ry"), None, None),
        P(("rx", "ry"), None, None),
        P(),
        P(("rx", "ry")),
        P(("rx", "ry"), None),
        P(("rx", "ry"), None),
    )
    return jax.shard_map(
        body,
        mesh=mesh,
        in_specs=placed,
        out_specs=(P(("rx", "ry"), None, None), P(("rx", "ry"), None, None), P()),
        check_vma=False,
    )
```

```python
import functools

import jax
import jax.numpy as jnp
from jax import lax
from jax.experimental import pallas as pl
from jax.experimental.pallas import tpu as pltpu
from jax.sharding import PartitionSpec as P

MESH = pl.DeviceIdType.MESH
F32, BF16 = jnp.float32, jnp.bfloat16


def dot(x, y):
    return jnp.dot(x, y, preferred_element_type=F32)


def low_lanes(shape):
    return lax.broadcasted_iota(jnp.int32, shape, len(shape) - 1) < 64


def put_window(ref, g, at, mid, low, high):
    rows = mid.shape[0] * 8
    mid, low, high = (v.reshape(rows, 128) for v in (mid, low, high))
    first = low_lanes((rows, 128))
    ref[g, at : at + rows, 0:128] = jnp.where(first, low, pltpu.roll(mid, 64, 1)).astype(BF16)
    ref[g, at : at + rows, 128:256] = high.astype(BF16)
    ref[g, at : at + rows, 256:384] = jnp.where(first, pltpu.roll(low, 64, 1), mid).astype(BF16)


def main_kernel(
    n_rx, n_ry, scale, conv_at,
    live_hbm, list_hbm, nb_hbm, feat_hbm, grad_hbm, w_hbm,
    out_ref, gf_ref, whole,
    live_ref, list_ref, nb_ref, feat_ref, grad_ref, w_ref, load_sem,
    t_ref, face_ref, recv_ref, wf_ref, wb_ref, xm_ref, xy_ref, lhs_ref, lhsx_ref, lhsf_ref, acc,
    dw, got0, src1, got1, src2, got2,
    face_send, face_recv, send0, send1, send2, send3, send4, send5,
    sem0, sem1, sem2, sem3, sem4, sem5,
):
    slots = feat_ref.shape[0]
    cap = recv_ref.shape[1]
    total_rows = dw.shape[0] * dw.shape[1] * dw.shape[2] * dw.shape[3]
    loads = [
        pltpu.make_async_copy(src, dst, load_sem.at[n])
        for n, (src, dst) in enumerate(
            (
                (feat_hbm, feat_ref), (grad_hbm, grad_ref), (live_hbm, live_ref),
                (list_hbm, list_ref), (nb_hbm, nb_ref), (w_hbm, w_ref),
            )
        )
    ]
    for x in loads:
        x.start()
    row, col = lax.axis_index("rx"), lax.axis_index("ry")
    half, par = n_ry // 2, lax.rem(col, 2)
    me = col // 2
    partner = (row, me * 2 + 1 - par)
    others = [lax.rem(me + d, half) for d in range(1, half)]
    rows = [lax.rem(row + d, n_rx) for d in range(1, n_rx)]
    sides = [
        (row > 0, (row - 1, col)),
        (row < n_rx - 1, (row + 1, col)),
        (col > 0, (row, col - 1)),
        (col < n_ry - 1, (row, col + 1)),
    ]

    barrier = pltpu.get_barrier_semaphore()
    for d in range(1, n_ry):
        peer = (row, lax.rem(col + d, n_ry))
        pl.semaphore_signal(barrier, inc=1, device_id=peer, device_id_type=MESH)
    for r in rows:
        pl.semaphore_signal(barrier, inc=1, device_id=(r, col), device_id_type=MESH)

    for x in loads[:5]:
        x.wait()

    def pack(g, carry):
        both = jnp.concatenate([feat_ref[g], grad_ref[g]], axis=0).astype(F32)
        cells = jnp.where(g < live_ref[0], jnp.transpose(both), 0.0)
        t_ref[g] = cells.reshape(8, 8, 8, 128)
        return carry

    lax.fori_loop(0, slots, pack, 0)
    for t in range(4):
        for k in range(cap):
            slot = list_ref[t, k]
            e = jnp.maximum(slot, 0)
            if t < 2:
                face = t_ref[e, 0 if t == 0 else 7]
            else:
                face = t_ref[e, :, 0 if t == 2 else 7]
            face = jnp.where(slot >= 0, face, 0.0)
            face_ref[t, k] = face.reshape(64, 128).astype(BF16)
    pl.semaphore_wait(barrier, n_ry + n_rx - 2)

    def copy(src, dst, ssem, rsem, peer):
        return pltpu.make_async_remote_copy(
            src_ref=src, dst_ref=dst, send_sem=ssem, recv_sem=rsem,
            device_id=peer, device_id_type=MESH,
        )

    def swap(t, into, peer):
        return copy(face_ref.at[t], recv_ref.at[into], face_send.at[t], face_recv.at[into], peer)

    for t, (there, peer) in enumerate(sides):

        @pl.when(there)
        def _():
            swap(t, t ^ 1, peer).start()

        @pl.when(jnp.logical_not(there))
        def _():
            recv_ref[t] = jnp.zeros(recv_ref.shape[1:], recv_ref.dtype)

    acc[...] = jnp.zeros_like(acc)
    xy_ref[...] = jnp.zeros_like(xy_ref)
    level = lax.broadcasted_iota(jnp.int32, (64, 8, 128), 1)

    def inner(p, carry):
        lane = lax.broadcasted_iota(jnp.int32, (64, 512), 1) % 64
        edges = []
        for h in range(2):
            g = 2 * p + h
            grads = jnp.where(g < live_ref[0], grad_ref[g].astype(F32), 0.0)

            def turned(shift):
                cut = [grads[:, 128 * q : 128 * q + 128] for q in range(4)]
                return jnp.concatenate([pltpu.roll(v, shift, 1) for v in cut], axis=1)

            ahead = jnp.where(lane < 56, turned(120), 0.0)
            behind = jnp.where(lane >= 8, turned(8), 0.0)
            lhs = jnp.concatenate([ahead, grads, behind], axis=0)
            lhs_ref[g] = lhs.astype(BF16)
            edges.append((lhs[:, 0:128], lhs[:, 384:512]))
            own = t_ref[g]
            ends = jnp.concatenate([own[:, 0:1], own[:, 7:8]], axis=1).reshape(128, 128)
            ends = jnp.transpose(ends)[64:128]
            which = lax.broadcasted_iota(jnp.int32, (64, 128), 1) % 16 < 8
            lhsf_ref[g] = jnp.concatenate(
                [jnp.where(which, ends, 0.0), jnp.where(which, 0.0, ends)], axis=0
            ).astype(BF16)

            mid = own.reshape(64, 8, 128)
            below, above = nb_ref[g, 4], nb_ref[g, 5]
            under = t_ref[jnp.clip(below, 0, slots - 1)].reshape(64, 8, 128)
            over = t_ref[jnp.clip(above, 0, slots - 1)].reshape(64, 8, 128)
            under = jnp.where(below >= 0, under, 0.0)
            over = jnp.where(above >= 0, over, 0.0)
            low = pltpu.roll(jnp.where(level == 7, under, mid), 1, 1)
            high = pltpu.roll(jnp.where(level == 0, over, mid), 7, 1)
            put_window(xm_ref, g, 64, mid, low, high)
            xm_ref[g, 0:64] = jnp.zeros((64, 384), BF16)
            xm_ref[g, 576:640] = jnp.zeros((64, 384), BF16)
            for a in range(3):
                acc[a] += dot(lhs_ref[g], xm_ref[g, 64 * a : 64 * a + 512, 0:256])
        first = low_lanes((192, 128))
        (low0, low1), (high0, high1) = edges
        lhsx_ref[0, p] = jnp.where(first, low0, pltpu.roll(high0, 64, 1)).astype(BF16)
        lhsx_ref[1, p] = jnp.where(first, pltpu.roll(low1, 64, 1), high1).astype(BF16)
        return carry

    lax.fori_loop(0, slots // 2, inner, 0)

    for t, (there, peer) in enumerate(sides):

        @pl.when(there)
        def _():
            swap(t, t ^ 1, peer).wait_send()
            swap(t, t, peer).wait_recv()

    def faces(g, carry):
        got = []
        for s in range(4):
            entry = nb_ref[g, s]
            e = jnp.clip(entry, 0, slots - 1)
            k = jnp.maximum(entry - slots, 0) % cap
            layer = 7 if s % 2 == 0 else 0
            local = t_ref[e, layer] if s < 2 else t_ref[e, :, layer]
            far = recv_ref[s, k].astype(F32).reshape(8, 8, 128)
            got.append(jnp.where(entry >= slots, far, jnp.where(entry >= 0, local, 0.0)))

        def around(mid):
            at = lax.broadcasted_iota(jnp.int32, mid.shape, 1)
            low = pltpu.roll(jnp.where(at == 7, 0.0, mid), 1, 1)
            high = pltpu.roll(jnp.where(at == 0, 0.0, mid), 7, 1)
            return mid, low, high

        put_window(xm_ref, g, 0, *around(got[0]))
        put_window(xm_ref, g, 576, *around(got[1]))
        both = jnp.concatenate([got[2][:, None], got[3][:, None]], axis=1).reshape(16, 8, 128)
        put_window(xy_ref, g, 16, *around(both))
        return carry

    lax.fori_loop(0, slots, faces, 0)

    pairs = slots // 2
    for s, a, at in ((0, 0, 0), (1, 2, 576)):
        lhs = jnp.concatenate([lhsx_ref[s, p] for p in range(pairs)], axis=1)
        rhs = jnp.concatenate([xm_ref[g, at : at + 64, 0:256] for g in range(slots)], axis=0)
        acc[a] += dot(lhs, rhs)
    lhs = jnp.concatenate([lhsf_ref[g] for g in range(slots)], axis=1)
    for a in range(3):
        rhs = [xy_ref[g, 16 * a : 16 * a + 128, 0:256] for g in range(slots)]
        more = dot(lhs, jnp.concatenate(rhs, axis=0))
        acc[a, 0:64] += more[0:64]
        acc[a, 128:192] += more[64:128]

    flat = acc[...].reshape(576, 256)
    rest = jnp.concatenate([flat[320:576, 128:256], jnp.zeros((64, 128), F32)], axis=0)
    third = jnp.where(low_lanes((320, 128)), flat[0:320, 128:256], pltpu.roll(rest, 64, 1))
    flat = [flat[:, 0:128], third]
    if total_rows > 896:
        flat.append(jnp.zeros((total_rows - 896, 128), F32))
    dw[...] = jnp.concatenate(flat, axis=0).reshape(dw.shape)

    def conv(g, carry):
        yf = yb = zf = zb = None
        for a in range(3):
            m = xm_ref[g, 64 * a : 64 * a + 512]
            y = xy_ref[g, 16 * a : 16 * a + 128]
            new = [
                dot(m[:, 0:256], wf_ref[a]), dot(m[:, 128:384], wb_ref[a]),
                dot(y[:, 0:256], wf_ref[a]), dot(y[:, 128:384], wb_ref[a]),
            ]
            if a:
                yf, yb, zf, zb = yf + new[0], yb + new[1], zf + new[2], zb + new[3]
            else:
                yf, yb, zf, zb = new
        yf, yb = yf.reshape(8, 8, 8, 256), yb.reshape(8, 8, 8, 256)
        zf, zb = zf.reshape(8, 2, 8, 256), zb.reshape(8, 2, 8, 256)

        def before(y, z):
            return jnp.concatenate([z[:, 0:1, :, 0:128], y[:, 0:7, :, 0:128]], axis=1)

        def after(y, z):
            return jnp.concatenate([y[:, 1:8, :, 128:256], z[:, 1:2, :, 128:256]], axis=1)

        first = low_lanes((8, 8, 8, 128))
        swapped = jnp.where(first, yb[..., 0:128], yf[..., 0:128])
        total = jnp.where(first, before(yf, zf), before(yb, zb))
        total += after(yf, zf) + after(yb, zb)
        total = total.reshape(512, 128) + pltpu.roll(swapped.reshape(512, 128), 64, 1)
        total = jnp.where(g < live_ref[0], total, 0.0)
        flat = jnp.transpose(total).astype(BF16)
        out_ref[g] = flat[0:64]
        gf_ref[g] = flat[64:128]
        return carry

    def run(n):
        lo, hi = conv_at[n], conv_at[n + 1]
        if hi > lo:
            lax.fori_loop(lo, hi, conv, 0)

    mid_rows = (n_rx // 2 - 1, n_rx // 2)
    far = jnp.where(row <= mid_rows[0], 1, 0)
    near = 1 - far
    row_of = {0: jnp.where(far == 1, mid_rows[1], mid_rows[0])}
    row_of[1] = mid_rows[0] + mid_rows[1] - row_of[0]
    share = (far, near)

    def pair(h):
        return copy(dw.at[h, 1 - par], got0.at[h], send0.at[h], sem0.at[h], partner)

    def along(h, c, into):
        peer = (row, 2 * c + par)
        return copy(src1.at[h, c], got1.at[h, into], send1.at[h, c], sem1.at[h, into], peer)

    def gather(n, source):
        return copy(src2.at[n], got2.at[source], send2.at[n], sem2.at[source], (row_of[n], col))

    def spread(h, r):
        at = whole.at[h, par, me]
        return copy(at, at, send3.at[r], sem3.at[h], (r, col))

    def fan(h, c, m):
        at = whole.at[h, par, m]
        return copy(at, at, send4.at[h, c], sem4.at[h, m], (row, 2 * c + par))

    def cross(h, m, parity):
        at = whole.at[h, parity, m]
        return copy(at, at, send5.at[h, m], sem5.at[h, m], partner)

    for h in share:
        pair(h).start()
    loads[5].wait()
    gap = jnp.zeros((64, 64), F32)
    wide = jnp.zeros((64, 256), BF16)
    for a in range(3):
        wf_ref[a, 192:256] = wide
        wb_ref[a, 0:64] = wide
        for c in range(3):
            front = [w_ref[9 * a + 3 * b + c].astype(F32) for b in range(3)]
            block = jnp.transpose(jnp.concatenate(front + [gap], axis=0))
            wf_ref[a, 64 * c : 64 * c + 64] = block.astype(BF16)
            back = [w_ref[26 - 9 * a - 3 * b - c].astype(F32) for b in range(3)]
            block = jnp.concatenate([back[1], back[0], gap, back[2]], axis=1)
            at = 64 * (2, 3, 1)[c]
            wb_ref[a, at : at + 64] = block.astype(BF16)
    run(0)
    for h in share:
        pair(h).wait_recv()
        src1[h] = dw[h, par] + got0[h]
        for c in others:
            along(h, c, me).start()
    for n, h in enumerate(share):
        run(1 + n)
        mine = src1[h, me]
        for c in reversed(others):
            along(h, c, c).wait_recv()
            mine += got1[h, c]
        src2[n] = mine
        if n == 0:
            gather(0, row).start()
    owner = row == row_of[1]

    @pl.when(jnp.logical_not(owner))
    def _():
        gather(1, row).start()

    run(3)

    @pl.when(owner)
    def _():
        mine = src2[1]
        for r in reversed(rows):
            gather(1, r).wait_recv()
            mine += got2[r]
        whole[near, par, me] = (mine * scale).astype(whole.dtype)
        for r in rows:
            spread(near, r).start()

    @pl.when(jnp.logical_not(owner))
    def _():
        spread(near, row).wait_recv()

    def onward(h):
        for c in others:
            fan(h, c, me).start()
        cross(h, me, par).start()

    onward(near)
    run(4)
    spread(far, row).wait_recv()
    onward(far)
    run(5)
    for h in (near, far):
        for c in reversed(others):
            fan(h, c, c).wait_recv()
            cross(h, c, par).start()
    for h in (near, far):
        for c in [me] + others:
            cross(h, c, 1 - par).wait_recv()

    for n, h in enumerate(share):
        pair(h).wait_send()
        for c in others:
            along(h, c, me).wait_send()
            fan(h, c, me).wait_send()
            cross(h, c, par).wait_send()
        cross(h, me, par).wait_send()
    gather(0, row).wait_send()

    @pl.when(jnp.logical_not(owner))
    def _():
        gather(1, row).wait_send()

    @pl.when(owner)
    def _():
        for r in rows:
            spread(near, r).wait_send()


def finish_kernel(packed_ref, out_ref, gf_ref, dw_hbm, out_hbm, gf_hbm, dw_ref, sem):
    copies = [
        pltpu.make_async_copy(out_ref, out_hbm, sem.at[0]),
        pltpu.make_async_copy(gf_ref, gf_hbm, sem.at[1]),
    ]
    for x in copies:
        x.start()
    count = 1
    for extent in packed_ref.shape[:-1]:
        count *= extent
    full = packed_ref[...].astype(F32).reshape(count, 128)
    for n in range(9):
        pair = full[64 * n : 64 * n + 64]
        dw_ref[3 * n] = pair[:, 0:64]
        dw_ref[3 * n + 1] = pair[:, 64:128]
        at, half = 576 + 64 * (n % 5), 64 * (n // 5)
        dw_ref[3 * n + 2] = full[at : at + 64, half : half + 64]
        if n % 3 == 2:
            done = pl.ds(3 * n - 6, 9)
            x = pltpu.make_async_copy(dw_ref.at[done], dw_hbm.at[done], sem.at[2 + n // 3])
            x.start()
            copies.append(x)
    for x in copies:
        x.wait()


def held(x):
    return pltpu.with_memory_space_constraint(x, pltpu.MemorySpace.HBM)


def body(features, grad_out, weights, live_count, neighbor, send_list):
    slots, channels = features.shape[0], features.shape[1]
    cap = send_list.shape[1]
    n_rx, n_ry = lax.axis_size("rx"), lax.axis_size("ry")
    vmem = pl.BlockSpec(memory_space=pltpu.VMEM)
    hbm = pl.BlockSpec(memory_space=pltpu.MemorySpace.HBM)
    scale = (512.0 * slots * n_rx * n_ry) ** (-0.5)
    half = n_ry // 2
    unit = -(-896 // (n_ry * 16)) * 8
    dma = pltpu.SemaphoreType.DMA
    conv_at = [n * slots // 8 for n in (0, 0, 4, 5, 7, 8, 8)]

    output, grad_features, packed = pl.pallas_call(
        functools.partial(main_kernel, n_rx, n_ry, scale, conv_at),
        out_shape=(
            jax.ShapeDtypeStruct(features.shape, BF16),
            jax.ShapeDtypeStruct(features.shape, BF16),
            jax.ShapeDtypeStruct((2, 2, half, unit, 128), BF16),
        ),
        in_specs=[hbm] * 6,
        out_specs=(vmem, vmem, vmem),
        scratch_shapes=[
            pltpu.SMEM(live_count.shape, jnp.int32),
            pltpu.SMEM(send_list.shape, jnp.int32),
            pltpu.SMEM(neighbor.shape, jnp.int32),
            pltpu.VMEM(features.shape, BF16),
            pltpu.VMEM(features.shape, BF16),
            pltpu.VMEM(weights.shape, BF16),
            dma((6,)),
            pltpu.VMEM((slots, 8, 8, 8, 128), F32),
            pltpu.VMEM((4, cap, 64, 128), BF16),
            pltpu.VMEM((4, cap, 64, 128), BF16),
            pltpu.VMEM((3, 256, 256), BF16),
            pltpu.VMEM((3, 256, 256), BF16),
            pltpu.VMEM((slots, 640, 384), BF16),
            pltpu.VMEM((slots, 160, 384), BF16),
            pltpu.VMEM((slots, 192, 512), BF16),
            pltpu.VMEM((2, slots // 2, 192, 128), BF16),
            pltpu.VMEM((slots, 128, 128), BF16),
            pltpu.VMEM((3, 192, 256), F32),
            pltpu.VMEM((2, 2, half, unit, 128), F32),
            pltpu.VMEM((2, half, unit, 128), F32),
            pltpu.VMEM((2, half, unit, 128), F32),
            pltpu.VMEM((2, half, unit, 128), F32),
            pltpu.VMEM((2, unit, 128), F32),
            pltpu.VMEM((n_rx, unit, 128), F32),
            dma((4,)), dma((4,)),
            dma((2,)), dma((2, half)), dma((2,)), dma((n_rx,)), dma((2, half)), dma((2, half)),
            dma((2,)), dma((2, half)), dma((n_rx,)), dma((2,)), dma((2, half)), dma((2, half)),
        ],
        compiler_params=pltpu.CompilerParams(
            collective_id=0, has_side_effects=True, vmem_limit_bytes=40 << 20
        ),
        name="main",
    )(live_count, *(held(x) for x in (send_list, neighbor, features, grad_out, weights)))

    grad_weights, output, grad_features = pl.pallas_call(
        finish_kernel,
        out_shape=(
            jax.ShapeDtypeStruct((27, channels, channels), F32),
            jax.ShapeDtypeStruct(features.shape, BF16),
            jax.ShapeDtypeStruct(features.shape, BF16),
        ),
        in_specs=[vmem, vmem, vmem],
        out_specs=(hbm, hbm, hbm),
        scratch_shapes=[pltpu.VMEM((27, channels, channels), F32), dma((5,))],
        compiler_params=pltpu.CompilerParams(vmem_limit_bytes=8 << 20),
        name="finish",
    )(packed, output, grad_features)
    return output, grad_features, grad_weights


def solution(mesh):
    placed = (
        P(("rx", "ry"), None, None),
        P(("rx", "ry"), None, None),
        P(),
        P(("rx", "ry")),
        P(("rx", "ry"), None),
        P(("rx", "ry"), None),
    )
    return jax.shard_map(
        body,
        mesh=mesh,
        in_specs=placed,
        out_specs=(P(("rx", "ry"), None, None), P(("rx", "ry"), None, None), P()),
        check_vma=False,
    )
```
